256 devices in a mesh: node: 32 (over z, x), feat: 8 (over y, core).
Axes of the slice: x: 4, y: 4, z: 8, core: 2. Of those that a mesh axis runs over, the one named last changes fastest.
Arguments:
- out_grad: bfloat16 [256, 262144], P('feat', 'node'), may hold values from -6 to 6
- pre_act: bfloat16 [256, 262144], P('feat', 'node'), may hold values from -6 to 6
- in_act: bfloat16 [256, 262144], P(None, ('node', 'feat')), may hold values from -6 to 6
- weight: bfloat16 [256, 256], replicated, may hold values from -0.375 to 0.375
- tiles: bfloat16 [2048, 24, 128, 128], P('node'), may hold values from -0.4375 to 0.4375
- indices: int32 [2048, 24], P('node'), may hold values from 0 to 2047, as said below
- counts: int32 [2048], P('node'), may hold values from 1 to 24, as said below
Outputs:
- in_grad: bfloat16 [256, 262144], P(None, ('node', 'feat'))
- weight_grad: float32 [256, 256], replicated
The draws below stay inside these ranges and needn't reach their ends.
Inputs may be any that keep to these rules, and one draw needn't show every extreme that they name: `indices`: the 24 column blocks named by one row block are distinct; slots at or after the row block's count are ignored. Each node device has a cap between 2 and 24, and its row blocks' counts are at most that cap, except for one row block in the whole graph whose count is 24.
All inputs are finite; a program needn't handle non-finite values.
Results may differ from the reference program's by a relative error of at most 0.012.
Values may be sent and summed in bfloat16 or wider, within the bound.
No kernel may reach another device: no remote copies, remote signals or barrier semaphores. Data moves between devices by JAX's collectives and lax.ppermute only.
A program may use at most 192 MiB of HBM per device.

```python
import jax
import jax.numpy as jnp
from jax import lax

HID = 256
BLK = 128
KMAX = 24
RB_DEV = 64
NRB = 2048
NODES = 262144


def draw_indices(key, part):
    keys = jax.random.split(key, NRB)

    def one_row(row_key):
        return jax.random.permutation(row_key, NRB)[:KMAX].astype(jnp.int32)
    return jax.vmap(one_row)(keys)


def draw_counts(key, part):
    key_cap = jax.random.fold_in(key, 11)
    key_each = jax.random.fold_in(key, 23)
    key_where = jax.random.fold_in(key, 37)
    groups = NRB // RB_DEV
    caps = jax.random.randint(key_cap, (groups,), 2, KMAX + 1).astype(jnp.int32)
    caps_rows = jnp.repeat(caps, RB_DEV)
    counts = jax.random.randint(key_each, (NRB,), 1, caps_rows + 1).astype(jnp.int32)
    where_full = jax.random.randint(key_where, (), 0, NRB)
    positions = jnp.arange(NRB, dtype=jnp.int32)
    return jnp.where(positions == where_full, KMAX, counts).astype(jnp.int32)


def level_of(own_key, shape, shards, smallest, top_value):
    gain = 1.0
    for dim, blocks in shards:
        steps = jax.random.uniform(jax.random.fold_in(jax.random.fold_in(own_key, 6), dim), (blocks,), jnp.float32, smallest / len(shards), top_value / len(shards))
        gain = gain * jnp.repeat(jnp.exp(steps), shape[dim] // blocks).reshape((-1,) + (1,) * (len(shape) - 1 - dim))
    return gain


def centred(own_key, dims, spread, reach, shards=(), held_as=jnp.bfloat16):
    drawn = jax.random.normal(own_key, dims, jnp.float32) * spread
    if len(shards) > 0:
        drawn = level_of(own_key, dims, shards, -0.22, 0.18) * drawn
    return jnp.clip(drawn, min=-reach, max=reach).astype(held_as)


def setup_inputs(seed: int = 0) -> dict:
    key_list = jax.random.split(jax.random.key(seed), 8)
    return {
        "out_grad": centred(key_list[0], (HID, NODES), 1.0, 6.0, ((0, 8), (1, 32))),
        "pre_act": centred(key_list[1], (HID, NODES), 1.0, 6.0, ((0, 8), (1, 32))),
        "in_act": centred(key_list[2], (HID, NODES), 1.0, 6.0, ((1, 256),)),
        "weight": centred(key_list[3], (HID, HID), HID ** -0.5, 0.375),
        "tiles": centred(key_list[4], (NRB, KMAX, BLK, BLK), ((BLK * KMAX / 2.5) ** -0.5), 0.4375, ((0, 32),)),
        "indices": draw_indices(jax.random.fold_in(key_list[7], 71), 0),
        "counts": draw_counts(jax.random.fold_in(key_list[7], 71), 0),
    }


def reference(out_grad, pre_act, in_act, weight, tiles, indices, counts):
    grad_pre = jnp.where(pre_act > 0, out_grad, jnp.zeros_like(out_grad))
    blocks = grad_pre.reshape(HID, NRB, BLK)
    slots = jnp.arange(KMAX, dtype=jnp.int32)

    def one_block(items):
        tile, index_row, count = items
        picked = jnp.take(blocks, index_row.astype(jnp.int32), axis=1).astype(jnp.float32)
        live = (slots < count).astype(jnp.float32)
        picked = picked * live[None, :, None]
        return jnp.einsum("fkc,kic->fi", picked, tile.astype(jnp.float32))

    summed = lax.map(one_block, (tiles, indices, counts))
    aggregated = summed.transpose(1, 0, 2).reshape(HID, NODES).astype(jnp.bfloat16)
    in_grad = jnp.dot(weight, aggregated, preferred_element_type=jnp.float32).astype(jnp.bfloat16)
    scale = float(NODES) ** -0.5
    weight_grad = lax.dot_general(in_act, aggregated, (((1,), (1,)), ((), ())), preferred_element_type=jnp.float32) * scale
    return in_grad, weight_grad
```

```python
import collections
import functools

import jax
import jax.numpy as jnp
from jax import lax
from jax.experimental import pallas as pl
from jax.experimental.pallas import tpu as pltpu
from jax.sharding import PartitionSpec as P


RING = (8, 4)
SPLIT = 38

QUAD = 4
GROUP = 8
DEPTH = 4


def plan_kernel(counts, work, length):
    rows = counts.shape[0]

    def one_row(r, n):
        runs = (counts[r] + QUAD - 1) // QUAD

        def one_run(c, n):
            work[n] = r * 32 + c * QUAD
            return n + 1

        return lax.fori_loop(0, runs, one_run, n)

    n = lax.fori_loop(0, rows, one_row, 0)
    length[0] = n
    for j in range(GROUP):
        work[n + j] = rows * 32


def make_plan(counts, slots):
    rows = counts.shape[0]
    smem = pl.BlockSpec(memory_space=pltpu.SMEM)
    return pl.pallas_call(
        plan_kernel,
        out_shape=(
            jax.ShapeDtypeStruct((rows * slots // QUAD + GROUP,), jnp.int32),
            jax.ShapeDtypeStruct((1,), jnp.int32),
        ),
        in_specs=[smem],
        out_specs=(smem, smem),
        name="plan",
    )(counts)


def gather_kernel(
    runs, here, work, length, counts, indices, tiles, *rest
):
    pieces = rest[: len(runs)]
    by_part, flat, held, stream, total, held_sem, stream_sem = rest[len(runs) :]
    rows, blk = counts.shape[0], tiles.shape[1]
    slots = tiles.shape[0] // rows
    groups = (length[0] + GROUP - 1) // GROUP
    shard = held.shape[0] // (RING[0] * RING[1])
    for piece, inside in zip(pieces, runs):
        start = 0
        for n, dz, dx, at in inside:
            z = lax.rem(here[1] + dz % RING[0], RING[0])
            x = lax.rem(here[2] + dx % RING[1], RING[1])
            place = (z * RING[1] + x) * shard + at
            pltpu.make_async_copy(
                piece.at[pl.ds(start, n)], held.at[pl.ds(place, n)], held_sem
            ).start()
            start += n

    def fetch(group):
        slot = lax.rem(group, DEPTH)
        for j in range(GROUP):
            entry = work[group * GROUP + j]
            r = jnp.minimum(lax.shift_right_logical(entry, 5), rows - 1)
            k = entry & 31
            pltpu.make_async_copy(
                tiles.at[pl.ds(r * slots + k, QUAD)], stream.at[slot, pl.ds(j * QUAD, QUAD)], stream_sem.at[slot]
            ).start()

    for g in range(DEPTH - 1):
        @pl.when(g < groups)
        def _():
            fetch(g)

    total[...] = jnp.zeros_like(total)
    pltpu.make_async_copy(held, held, held_sem).wait()

    def one_group(group, carry):
        @pl.when(group + DEPTH - 1 < groups)
        def _():
            fetch(group + DEPTH - 1)

        slot = lax.rem(group, DEPTH)
        pltpu.make_async_copy(
            tiles.at[pl.ds(0, GROUP * QUAD)], stream.at[slot], stream_sem.at[slot]
        ).wait()
        terms, where = [], []
        for j in range(GROUP):
            entry = work[group * GROUP + j]
            r = lax.shift_right_logical(entry, 5)
            k = entry & 31
            row = jnp.minimum(r, rows - 1)
            live = jnp.where(r < rows, counts[row], 0)
            picked = []
            for q in range(QUAD):
                block = held[indices[row * slots + k + q]]
                picked.append(jnp.where(k + q < live, block, jnp.zeros_like(block)))
            picked = jnp.concatenate(picked, axis=1)
            weights = jnp.concatenate([stream[slot, j * QUAD + q] for q in range(QUAD)], axis=1)
            terms.append(
                lax.dot_general(
                    picked, weights, (((1,), (1,)), ((), ())), preferred_element_type=jnp.float32
                )
            )
            where.append(r)
        for j in range(GROUP):
            total[where[j]] += terms[j]
        return carry

    lax.fori_loop(0, groups, one_group, 0)

    parts, nodes = by_part.shape[0], by_part.shape[2]
    per_part = nodes // blk

    def one_part(s, carry):
        part = lax.rem(here[0] + s, parts)
        for i in range(per_part):
            value = total[part * per_part + i].astype(jnp.bfloat16)
            by_part[s, :, i * blk : (i + 1) * blk] = value
            flat[:, pl.ds(pl.multiple_of(s * nodes + i * blk, blk), blk)] = value
        return carry

    lax.fori_loop(0, parts, one_part, 0)


def gathered_sum(here, counts, indices, tiles, pieces, parts):
    rows, slots, blk, _ = tiles.shape
    feats = pieces[0].blocks.shape[1]
    total_blocks = sum(p.blocks.shape[0] for p in pieces)
    smem = pl.BlockSpec(memory_space=pltpu.SMEM)
    vmem = pl.BlockSpec(memory_space=pltpu.VMEM)
    anywhere = pl.BlockSpec(memory_space=pl.ANY)
    out_shape = (
        jax.ShapeDtypeStruct((parts, feats, rows * blk // parts), jnp.bfloat16),
        jax.ShapeDtypeStruct((feats, rows * blk), jnp.bfloat16),
    )
    work, length = make_plan(counts, slots)
    work_done = rows * slots // 2
    return pl.pallas_call(
        functools.partial(gather_kernel, [p.runs for p in pieces]),
        out_shape=out_shape,
        in_specs=[smem] * 5 + [anywhere] * (1 + len(pieces)),
        out_specs=(vmem, vmem),
        scratch_shapes=[
            pltpu.VMEM((total_blocks, feats, blk), pieces[0].blocks.dtype),
            pltpu.VMEM((DEPTH, GROUP * QUAD, blk, blk), tiles.dtype),
            pltpu.VMEM((rows + 1, feats, blk), jnp.float32),
            pltpu.SemaphoreType.DMA,
            pltpu.SemaphoreType.DMA((DEPTH,)),
        ],
        compiler_params=pltpu.CompilerParams(vmem_limit_bytes=48 * 1024 * 1024),
        cost_estimate=pl.CostEstimate(
            flops=2 * work_done * feats * blk * blk,
            bytes_accessed=2 * work_done * blk * blk + 2 * total_blocks * feats * blk,
            transcendentals=0,
        ),
        name="gathered_sum",
    )(
        here,
        work,
        length,
        counts,
        indices.reshape(-1),
        tiles.reshape(rows * slots, blk, blk),
        *(p.blocks for p in pieces),
    )


Piece = collections.namedtuple("Piece", "blocks runs")


def hop(piece, dz, dx):
    nz, nx = RING
    pairs = [
        (z * nx + x, (z + dz) % nz * nx + (x + dx) % nx) for z in range(nz) for x in range(nx)
    ]
    blocks = lax.ppermute(piece.blocks, "node", pairs)
    return Piece(blocks, [(n, z - dz, x - dx, at) for n, z, x, at in piece.runs])


def half(piece, upper):
    size = sum(run[0] for run in piece.runs)
    low, high = (size // 2, size) if upper else (0, size // 2)
    runs, seen = [], 0
    for n, z, x, at in piece.runs:
        first, last = max(low, seen), min(high, seen + n)
        if first < last:
            runs.append((last - first, z, x, at + first - seen))
        seen += n
    return Piece(piece.blocks[low:high], runs)


def join(*pieces):
    return Piece(
        jnp.concatenate([p.blocks for p in pieces], axis=0), [r for p in pieces for r in p.runs]
    )


def along(axis, piece, steps):
    dz, dx = (1, 0) if axis == "z" else (0, 1)
    up = down = piece
    out = []
    for s in range(1, steps + 1):
        if s == steps:
            up, down = half(up, False), half(down, True)
        up = hop(up, dz, dx)
        down = hop(down, -dz, -dx)
        out.append([up, down])
    return out


def gathered(own):
    a = Piece(own[:SPLIT], [(SPLIT, 0, 0, 0)])
    b = Piece(own[SPLIT:], [(own.shape[0] - SPLIT, 0, 0, SPLIT)])
    az = along("z", a, RING[0] // 2)
    bx = along("x", b, RING[1] // 2)
    first = join(*az[0], *az[1])
    second = join(*az[2], *az[3])
    across = join(b, *bx[0], *bx[1])
    pieces = [a, first, second, across]
    for piece in (a, first, second):
        for step in along("x", piece, RING[1] // 2):
            pieces += step
    for step in along("z", across, RING[0] // 2):
        pieces += step
    return pieces


def shifted(value, axis, shift):
    size = lax.axis_size(axis)
    return lax.ppermute(value, axis, [(i, (i + shift) % size) for i in range(size)])


def sent_to_all(shard, axis):
    size = lax.axis_size(axis)
    return lax.all_to_all(
        jnp.broadcast_to(shard[None], (size, *shard.shape)), axis, 0, 0, tiled=True
    )


def per_device(out_grad, pre_act, in_act, weight, tiles, indices, counts):
    feats, local_nodes = out_grad.shape
    _, _, blk, _ = tiles.shape
    parts, nodes = lax.axis_size("feat"), lax.axis_size("node")
    assert nodes == RING[0] * RING[1]
    grad_pre = jnp.where(pre_act > 0, out_grad, jnp.zeros_like(out_grad))
    own = grad_pre.reshape(feats, local_nodes // blk, blk).transpose(1, 0, 2)
    pieces = gathered(own)
    me = lax.axis_index("feat")
    spot = lax.axis_index("node")
    here = jnp.stack([me, spot // RING[1], spot % RING[1]]).astype(jnp.int32)
    acts = jnp.concatenate(
        [in_act] + [shifted(in_act, "feat", -s) for s in range(1, parts)], axis=1
    )
    turned = jnp.concatenate(
        [
            lax.dynamic_slice_in_dim(weight, lax.rem(me + parts - s, parts) * feats, feats, 1)
            for s in range(parts)
        ],
        axis=1,
    )
    by_part, flat = gathered_sum(here, counts, indices, tiles, pieces, parts)

    scale = float(local_nodes * nodes) ** (-0.5)
    column_part = (
        lax.dot_general(acts, flat, (((1,), (1,)), ((), ())), preferred_element_type=jnp.float32)
        * scale
    )
    everyone = sent_to_all(column_part.astype(jnp.bfloat16), "node")
    column = jnp.sum(everyone.astype(jnp.float32), axis=0)
    columns = sent_to_all(column.astype(jnp.bfloat16), "feat")
    weight_grad = columns.transpose(1, 0, 2).reshape(column.shape[0], -1).astype(jnp.float32)

    received = [by_part[0]] + [shifted(by_part[s], "feat", s) for s in range(1, parts)]
    node_rows = jnp.concatenate(received, axis=0)
    in_grad = jnp.dot(turned, node_rows, preferred_element_type=jnp.float32).astype(jnp.bfloat16)
    return in_grad, weight_grad


def solution(mesh):
    in_specs = (
        P("feat", "node"),
        P("feat", "node"),
        P(None, ("node", "feat")),
        P(),
        P("node", None, None, None),
        P("node", None),
        P("node"),
    )
    out_specs = (P(None, ("node", "feat")), P())

    return jax.shard_map(
        per_device, mesh=mesh, in_specs=in_specs, out_specs=out_specs, check_vma=False
    )
```

```python
import collections
import functools

import jax
import jax.numpy as jnp
from jax import lax
from jax.experimental import pallas as pl
from jax.experimental.pallas import tpu as pltpu
from jax.sharding import PartitionSpec as P


RING = (8, 4)
FEAT = (4, 2)
SPLIT = 38
GROUPS = [("gb", (1,), True), ("gc", (2,), False), ("gd", (3, 4), True)]
UPPER = 33

QUAD = 4
GROUP = 8
DEPTH = 4


def plan_kernel(counts, work, length):
    rows = counts.shape[0]

    def one_row(r, n):
        runs = (counts[r] + QUAD - 1) // QUAD

        def one_run(c, n):
            work[n] = r * 32 + c * QUAD
            return n + 1

        return lax.fori_loop(0, runs, one_run, n)

    n = lax.fori_loop(0, rows, one_row, 0)
    length[0] = n
    for j in range(GROUP):
        work[n + j] = rows * 32


def make_plan(counts, slots):
    rows = counts.shape[0]
    smem = pl.BlockSpec(memory_space=pltpu.SMEM)
    return pl.pallas_call(
        plan_kernel,
        out_shape=(
            jax.ShapeDtypeStruct((rows * slots // QUAD + GROUP,), jnp.int32),
            jax.ShapeDtypeStruct((1,), jnp.int32),
        ),
        in_specs=[smem],
        out_specs=(smem, smem),
        name="plan",
    )(counts)


def gather_kernel(
    runs, scale, pairs, here, work, length, counts, indices, tiles, *rest
):
    pieces = rest[: len(runs)]
    acts = rest[len(runs) : len(runs) + pairs]
    keep, cross, column, held, stream, total, flat, acts_held, held_sem, stream_sem, acts_sem = rest[
        len(runs) + pairs :
    ]
    rows, blk = counts.shape[0], tiles.shape[1]
    slots = tiles.shape[0] // rows
    groups = (length[0] + GROUP - 1) // GROUP
    shard = held.shape[0] // (RING[0] * RING[1])
    for piece, inside in zip(pieces, runs):
        start = 0
        for n, dz, dx, at in inside:
            z = lax.rem(here[2] + dz % RING[0], RING[0])
            x = lax.rem(here[3] + dx % RING[1], RING[1])
            place = (z * RING[1] + x) * shard + at
            pltpu.make_async_copy(
                piece.at[pl.ds(start, n)], held.at[pl.ds(place, n)], held_sem
            ).start()
            start += n

    def fetch(group):
        slot = lax.rem(group, DEPTH)
        for j in range(GROUP):
            entry = work[group * GROUP + j]
            r = jnp.minimum(lax.shift_right_logical(entry, 5), rows - 1)
            k = entry & 31
            pltpu.make_async_copy(
                tiles.at[pl.ds(r * slots + k, QUAD)], stream.at[slot, pl.ds(j * QUAD, QUAD)], stream_sem.at[slot]
            ).start()

    def arrived(slot):
        pltpu.make_async_copy(
            tiles.at[pl.ds(0, GROUP * QUAD)], stream.at[slot], stream_sem.at[slot]
        ).wait()

    for g in range(DEPTH - 1):
        @pl.when(g < groups)
        def _():
            fetch(g)

    for s, pair in enumerate(acts):
        pltpu.make_async_copy(pair, acts_held.at[s], acts_sem).start()
    total[...] = jnp.zeros_like(total)
    pltpu.make_async_copy(held, held, held_sem).wait()

    def one_group(group, carry):
        @pl.when(group + DEPTH - 1 < groups)
        def _():
            fetch(group + DEPTH - 1)

        slot = lax.rem(group, DEPTH)
        arrived(slot)
        terms, where = [], []
        for j in range(GROUP):
            entry = work[group * GROUP + j]
            r = lax.shift_right_logical(entry, 5)
            k = entry & 31
            row = jnp.minimum(r, rows - 1)
            live = jnp.where(r < rows, counts[row], 0)
            picked = []
            for q in range(QUAD):
                block = held[indices[row * slots + k + q]]
                picked.append(jnp.where(k + q < live, block, jnp.zeros_like(block)))
            picked = jnp.concatenate(picked, axis=1)
            weights = jnp.concatenate([stream[slot, j * QUAD + q] for q in range(QUAD)], axis=1)
            terms.append(
                lax.dot_general(
                    picked, weights, (((1,), (1,)), ((), ())), preferred_element_type=jnp.float32
                )
            )
            where.append(r)
        for j in range(GROUP):
            total[where[j]] += terms[j]
        return carry

    lax.fori_loop(0, groups, one_group, 0)

    nodes = keep.shape[2]
    per_part = nodes // blk

    def one_step(s, carry):
        for c, out in enumerate((keep, cross)):
            part = lax.rem(here[0] + s, FEAT[0]) * FEAT[1] + lax.rem(here[1] + c, FEAT[1])
            for i in range(per_part):
                value = total[part * per_part + i].astype(jnp.bfloat16)
                out[s, :, i * blk : (i + 1) * blk] = value
                at = pl.multiple_of((s * FEAT[1] + c) * nodes + i * blk, blk)
                flat[:, pl.ds(at, blk)] = value
        return carry

    lax.fori_loop(0, FEAT[0], one_step, 0)
    pltpu.make_async_copy(acts_held, acts_held, acts_sem).wait()
    columns = None
    for s in range(FEAT[0]):
        for c in range(FEAT[1]):
            first = (s * FEAT[1] + c) * nodes
            term = lax.dot_general(
                flat[:, first : first + nodes],
                acts_held[s, c],
                (((1,), (1,)), ((), ())),
                preferred_element_type=jnp.float32,
            )
            columns = term if columns is None else columns + term
    columns = (columns * scale).astype(jnp.bfloat16)
    for i in range(column.shape[0]):
        column[i] = columns


def gathered_sum(here, counts, indices, tiles, pieces, acts, scale, parts, copies):
    rows, slots, blk, _ = tiles.shape
    feats = pieces[0].blocks.shape[1]
    total_blocks = sum(p.blocks.shape[0] for p in pieces)
    smem = pl.BlockSpec(memory_space=pltpu.SMEM)
    vmem = pl.BlockSpec(memory_space=pltpu.VMEM)
    anywhere = pl.BlockSpec(memory_space=pl.ANY)
    out_shape = (
        jax.ShapeDtypeStruct((FEAT[0], feats, rows * blk // parts), jnp.bfloat16),
        jax.ShapeDtypeStruct((FEAT[0], feats, rows * blk // parts), jnp.bfloat16),
        jax.ShapeDtypeStruct((copies, feats, acts[0].shape[1]), jnp.bfloat16),
    )
    work, length = make_plan(counts, slots)
    work_done = rows * slots // 2
    return pl.pallas_call(
        functools.partial(gather_kernel, [p.runs for p in pieces], scale, len(acts)),
        out_shape=out_shape,
        in_specs=[smem] * 5 + [anywhere] * (1 + len(pieces) + len(acts)),
        out_specs=(vmem, vmem, vmem),
        scratch_shapes=[
            pltpu.VMEM((total_blocks, feats, blk), pieces[0].blocks.dtype),
            pltpu.VMEM((DEPTH, GROUP * QUAD, blk, blk), tiles.dtype),
            pltpu.VMEM((rows + 1, feats, blk), jnp.float32),
            pltpu.VMEM((feats, rows * blk), jnp.bfloat16),
            pltpu.VMEM((len(acts), *acts[0].shape), acts[0].dtype),
            pltpu.SemaphoreType.DMA,
            pltpu.SemaphoreType.DMA((DEPTH,)),
            pltpu.SemaphoreType.DMA,
        ],
        compiler_params=pltpu.CompilerParams(vmem_limit_bytes=62 * 1024 * 1024),
        cost_estimate=pl.CostEstimate(
            flops=2 * work_done * feats * blk * blk,
            bytes_accessed=2 * work_done * blk * blk + 2 * total_blocks * feats * blk,
            transcendentals=0,
        ),
        name="gathered_sum",
    )(
        here,
        work,
        length,
        counts,
        indices.reshape(-1),
        tiles.reshape(rows * slots, blk, blk),
        *(p.blocks for p in pieces),
        *acts,
    )


Piece = collections.namedtuple("Piece", "blocks runs")


def hop(piece, dz, dx):
    nz, nx = RING
    pairs = [
        (z * nx + x, (z + dz) % nz * nx + (x + dx) % nx) for z in range(nz) for x in range(nx)
    ]
    blocks = lax.ppermute(piece.blocks, "node", pairs)
    return Piece(blocks, [(n, z - dz, x - dx, at) for n, z, x, at in piece.runs])


def cut(piece, low, high):
    runs, seen = [], 0
    for n, z, x, at in piece.runs:
        first, last = max(low, seen), min(high, seen + n)
        if first < last:
            runs.append((last - first, z, x, at + first - seen))
        seen += n
    return Piece(piece.blocks[low:high], runs)


def join(*pieces):
    return Piece(
        jnp.concatenate([p.blocks for p in pieces], axis=0), [r for p in pieces for r in p.runs]
    )


def along(axis, piece, steps, upper):
    dz, dx = (1, 0) if axis == "z" else (0, 1)
    up = down = piece
    size = piece.blocks.shape[0]
    out = []
    for s in range(1, steps + 1):
        if s == steps and upper < size:
            down = cut(down, upper, size) if upper else down
            up = cut(up, 0, upper) if upper else None
        elif s == steps:
            down = None
        step = []
        if up is not None:
            up = hop(up, dz, dx)
            step.append(up)
        if down is not None:
            down = hop(down, -dz, -dx)
            step.append(down)
        out.append(step)
    return out


def gathered(own):
    shard = own.shape[0]
    a = Piece(own[:SPLIT], [(SPLIT, 0, 0, 0)])
    b = Piece(own[SPLIT:], [(shard - SPLIT, 0, 0, SPLIT)])
    az = along("z", a, RING[0] // 2, SPLIT)
    bx = along("x", b, RING[1] // 2, shard - SPLIT)
    across = join(b, *bx[0], *bx[1])
    pieces = [a, across]
    groups = [("ga", a, False)]
    for name, steps, one_way in GROUPS:
        joined = join(*(p for s in steps for p in az[s - 1]))
        groups.append((name, joined, one_way))
        pieces.append(joined)
    for name, piece, one_way in groups:
        for step in along("x", piece, RING[1] // 2, piece.blocks.shape[0] if one_way else 0):
            pieces += step
    for step in along("z", across, RING[0] // 2, UPPER):
        pieces += step
    return pieces


def over_feat(value, steps, swap):
    ny, nc = FEAT
    pairs = [
        (y * nc + c, (y + steps) % ny * nc + (c + swap) % nc) for y in range(ny) for c in range(nc)
    ]
    return lax.ppermute(value, "feat", pairs)


def sent_to_all(shard, axis):
    size = lax.axis_size(axis)
    return lax.all_to_all(
        jnp.broadcast_to(shard[None], (size, *shard.shape)), axis, 0, 0, tiled=True
    )


def per_device(out_grad, pre_act, in_act, weight, tiles, indices, counts):
    feats, local_nodes = out_grad.shape
    _, _, blk, _ = tiles.shape
    parts, nodes = lax.axis_size("feat"), lax.axis_size("node")
    assert nodes == RING[0] * RING[1] and parts == FEAT[0] * FEAT[1]
    grad_pre = jnp.where(pre_act > 0, out_grad, jnp.zeros_like(out_grad))
    own = grad_pre.reshape(feats, local_nodes // blk, blk).transpose(1, 0, 2)
    pieces = gathered(own)
    me = lax.axis_index("feat")
    spot = lax.axis_index("node")
    y, core = me // FEAT[1], me % FEAT[1]
    here = jnp.stack([y, core, spot // RING[1], spot % RING[1]]).astype(jnp.int32)
    both = jnp.stack([in_act, over_feat(in_act, 0, 1)])
    acts = [both] + [over_feat(both, -s, 0) for s in range(1, FEAT[0])]
    turned = jnp.concatenate(
        [
            lax.dynamic_slice_in_dim(
                weight,
                (lax.rem(y + FEAT[0] - s, FEAT[0]) * FEAT[1] + lax.rem(core + c, FEAT[1])) * feats,
                feats,
                1,
            )
            for s in range(FEAT[0])
            for c in range(FEAT[1])
        ],
        axis=1,
    )
    scale = float(local_nodes * nodes) ** (-0.5)
    keep, cross, column = gathered_sum(
        here, counts, indices, tiles, pieces, acts, scale, parts, nodes
    )

    everyone = lax.all_to_all(column, "node", 0, 0, tiled=True)
    column = jnp.sum(everyone.astype(jnp.float32), axis=0)
    columns = sent_to_all(column.astype(jnp.bfloat16), "feat")
    weight_grad = columns.reshape(-1, column.shape[1]).T.astype(jnp.float32)

    crossed = over_feat(cross, 0, 1)
    ready = [jnp.concatenate([keep[s], crossed[s]], axis=0) for s in range(FEAT[0])]
    received = [ready[0]] + [over_feat(ready[s], s, 0) for s in range(1, FEAT[0])]
    node_rows = jnp.concatenate(received, axis=0)
    in_grad = jnp.dot(turned, node_rows, preferred_element_type=jnp.float32).astype(jnp.bfloat16)
    return in_grad, weight_grad


def solution(mesh):
    in_specs = (
        P("feat", "node"),
        P("feat", "node"),
        P(None, ("node", "feat")),
        P(),
        P("node", None, None, None),
        P("node", None),
        P("node"),
    )
    out_specs = (P(None, ("node", "feat")), P())

    return jax.shard_map(
        per_device, mesh=mesh, in_specs=in_specs, out_specs=out_specs, check_vma=False
    )
```

```python
import collections
import functools

import jax
import jax.numpy as jnp
from jax import lax
from jax.experimental import pallas as pl
from jax.experimental.pallas import tpu as pltpu
from jax.sharding import PartitionSpec as P


RING = (8, 4)
FEAT = (4, 2)
SPLIT = 38
GROUPS = [("gb", (1,), True), ("gc", (2,), False), ("gd", (3, 4), True)]
UPPER = 33

QUAD = 4
GROUP = 8
DEPTH = 4


def plan_kernel(counts, work, length):
    rows = counts.shape[0]

    def one_row(r, n):
        runs = (counts[r] + QUAD - 1) // QUAD

        def one_run(c, n):
            work[n] = r * 32 + c * QUAD
            return n + 1

        return lax.fori_loop(0, runs, one_run, n)

    n = lax.fori_loop(0, rows, one_row, 0)
    length[0] = n
    for j in range(GROUP):
        work[n + j] = rows * 32


def make_plan(counts, slots):
    rows = counts.shape[0]
    smem = pl.BlockSpec(memory_space=pltpu.SMEM)
    return pl.pallas_call(
        plan_kernel,
        out_shape=(
            jax.ShapeDtypeStruct((rows * slots // QUAD + GROUP,), jnp.int32),
            jax.ShapeDtypeStruct((1,), jnp.int32),
        ),
        in_specs=[smem],
        out_specs=(smem, smem),
        name="plan",
    )(counts)


def gather_kernel(
    runs, here, work, length, counts, indices, tiles, *rest
):
    pieces = rest[: len(runs)]
    keep, cross, flat, held, stream, total, held_sem, stream_sem = rest[len(runs) :]
    rows, blk = counts.shape[0], tiles.shape[1]
    slots = tiles.shape[0] // rows
    groups = (length[0] + GROUP - 1) // GROUP
    shard = held.shape[0] // (RING[0] * RING[1])
    for piece, inside in zip(pieces, runs):
        start = 0
        for n, dz, dx, at in inside:
            z = lax.rem(here[2] + dz % RING[0], RING[0])
            x = lax.rem(here[3] + dx % RING[1], RING[1])
            place = (z * RING[1] + x) * shard + at
            pltpu.make_async_copy(
                piece.at[pl.ds(start, n)], held.at[pl.ds(place, n)], held_sem
            ).start()
            start += n

    def fetch(group):
        slot = lax.rem(group, DEPTH)
        for j in range(GROUP):
            entry = work[group * GROUP + j]
            r = jnp.minimum(lax.shift_right_logical(entry, 5), rows - 1)
            k = entry & 31
            pltpu.make_async_copy(
                tiles.at[pl.ds(r * slots + k, QUAD)], stream.at[slot, pl.ds(j * QUAD, QUAD)], stream_sem.at[slot]
            ).start()

    for g in range(DEPTH - 1):
        @pl.when(g < groups)
        def _():
            fetch(g)

    total[...] = jnp.zeros_like(total)
    pltpu.make_async_copy(held, held, held_sem).wait()

    def one_group(group, carry):
        @pl.when(group + DEPTH - 1 < groups)
        def _():
            fetch(group + DEPTH - 1)

        slot = lax.rem(group, DEPTH)
        pltpu.make_async_copy(
            tiles.at[pl.ds(0, GROUP * QUAD)], stream.at[slot], stream_sem.at[slot]
        ).wait()
        terms, where = [], []
        for j in range(GROUP):
            entry = work[group * GROUP + j]
            r = lax.shift_right_logical(entry, 5)
            k = entry & 31
            row = jnp.minimum(r, rows - 1)
            live = jnp.where(r < rows, counts[row], 0)
            picked = []
            for q in range(QUAD):
                block = held[indices[row * slots + k + q]]
                picked.append(jnp.where(k + q < live, block, jnp.zeros_like(block)))
            picked = jnp.concatenate(picked, axis=1)
            weights = jnp.concatenate([stream[slot, j * QUAD + q] for q in range(QUAD)], axis=1)
            terms.append(
                lax.dot_general(
                    picked, weights, (((1,), (1,)), ((), ())), preferred_element_type=jnp.float32
                )
            )
            where.append(r)
        for j in range(GROUP):
            total[where[j]] += terms[j]
        return carry

    lax.fori_loop(0, groups, one_group, 0)

    nodes = keep.shape[2]
    per_part = nodes // blk

    def one_step(s, carry):
        for c, out in enumerate((keep, cross)):
            part = lax.rem(here[0] + s, FEAT[0]) * FEAT[1] + lax.rem(here[1] + c, FEAT[1])
            for i in range(per_part):
                value = total[part * per_part + i].astype(jnp.bfloat16)
                out[s, :, i * blk : (i + 1) * blk] = value
                at = pl.multiple_of((s * FEAT[1] + c) * nodes + i * blk, blk)
                flat[:, pl.ds(at, blk)] = value
        return carry

    lax.fori_loop(0, FEAT[0], one_step, 0)


def gathered_sum(here, counts, indices, tiles, pieces, parts):
    rows, slots, blk, _ = tiles.shape
    feats = pieces[0].blocks.shape[1]
    total_blocks = sum(p.blocks.shape[0] for p in pieces)
    smem = pl.BlockSpec(memory_space=pltpu.SMEM)
    vmem = pl.BlockSpec(memory_space=pltpu.VMEM)
    anywhere = pl.BlockSpec(memory_space=pl.ANY)
    out_shape = (
        jax.ShapeDtypeStruct((FEAT[0], feats, rows * blk // parts), jnp.bfloat16),
        jax.ShapeDtypeStruct((FEAT[0], feats, rows * blk // parts), jnp.bfloat16),
        jax.ShapeDtypeStruct((feats, rows * blk), jnp.bfloat16),
    )
    work, length = make_plan(counts, slots)
    work_done = rows * slots // 2
    return pl.pallas_call(
        functools.partial(gather_kernel, [p.runs for p in pieces]),
        out_shape=out_shape,
        in_specs=[smem] * 5 + [anywhere] * (1 + len(pieces)),
        out_specs=(vmem, vmem, vmem),
        scratch_shapes=[
            pltpu.VMEM((total_blocks, feats, blk), pieces[0].blocks.dtype),
            pltpu.VMEM((DEPTH, GROUP * QUAD, blk, blk), tiles.dtype),
            pltpu.VMEM((rows + 1, feats, blk), jnp.float32),
            pltpu.SemaphoreType.DMA,
            pltpu.SemaphoreType.DMA((DEPTH,)),
        ],
        compiler_params=pltpu.CompilerParams(vmem_limit_bytes=48 * 1024 * 1024),
        cost_estimate=pl.CostEstimate(
            flops=2 * work_done * feats * blk * blk,
            bytes_accessed=2 * work_done * blk * blk + 2 * total_blocks * feats * blk,
            transcendentals=0,
        ),
        name="gathered_sum",
    )(
        here,
        work,
        length,
        counts,
        indices.reshape(-1),
        tiles.reshape(rows * slots, blk, blk),
        *(p.blocks for p in pieces),
    )


Piece = collections.namedtuple("Piece", "blocks runs")


def hop(piece, dz, dx):
    nz, nx = RING
    pairs = [
        (z * nx + x, (z + dz) % nz * nx + (x + dx) % nx) for z in range(nz) for x in range(nx)
    ]
    blocks = lax.ppermute(piece.blocks, "node", pairs)
    return Piece(blocks, [(n, z - dz, x - dx, at) for n, z, x, at in piece.runs])


def cut(piece, low, high):
    runs, seen = [], 0
    for n, z, x, at in piece.runs:
        first, last = max(low, seen), min(high, seen + n)
        if first < last:
            runs.append((last - first, z, x, at + first - seen))
        seen += n
    return Piece(piece.blocks[low:high], runs)


def join(*pieces):
    return Piece(
        jnp.concatenate([p.blocks for p in pieces], axis=0), [r for p in pieces for r in p.runs]
    )


def along(axis, piece, steps, upper):
    dz, dx = (1, 0) if axis == "z" else (0, 1)
    up = down = piece
    size = piece.blocks.shape[0]
    out = []
    for s in range(1, steps + 1):
        if s == steps and upper < size:
            down = cut(down, upper, size) if upper else down
            up = cut(up, 0, upper) if upper else None
        elif s == steps:
            down = None
        step = []
        if up is not None:
            up = hop(up, dz, dx)
            step.append(up)
        if down is not None:
            down = hop(down, -dz, -dx)
            step.append(down)
        out.append(step)
    return out


def gathered(own):
    shard = own.shape[0]
    a = Piece(own[:SPLIT], [(SPLIT, 0, 0, 0)])
    b = Piece(own[SPLIT:], [(shard - SPLIT, 0, 0, SPLIT)])
    az = along("z", a, RING[0] // 2, SPLIT)
    bx = along("x", b, RING[1] // 2, shard - SPLIT)
    across = join(b, *bx[0], *bx[1])
    pieces = [a, across]
    groups = [("ga", a, False)]
    for name, steps, one_way in GROUPS:
        joined = join(*(p for s in steps for p in az[s - 1]))
        groups.append((name, joined, one_way))
        pieces.append(joined)
    for name, piece, one_way in groups:
        for step in along("x", piece, RING[1] // 2, piece.blocks.shape[0] if one_way else 0):
            pieces += step
    for step in along("z", across, RING[0] // 2, UPPER):
        pieces += step
    return pieces


def over_feat(value, steps, swap):
    ny, nc = FEAT
    pairs = [
        (y * nc + c, (y + steps) % ny * nc + (c + swap) % nc) for y in range(ny) for c in range(nc)
    ]
    return lax.ppermute(value, "feat", pairs)


def column_kernel(scale, *refs):
    acts, flat, out, held, sems = refs[:-4], refs[-4], refs[-3], refs[-2], refs[-1]
    nodes = acts[0].shape[2]
    total = None
    loads = [
        pltpu.make_async_copy(pair, held.at[s], sems.at[s]) for s, pair in enumerate(acts)
    ]
    for load in loads:
        load.start()
    for s in range(len(acts) * acts[0].shape[0]):
        pair, c = s // acts[0].shape[0], s % acts[0].shape[0]
        if c == 0:
            loads[pair].wait()
        term = lax.dot_general(
            flat[:, s * nodes : (s + 1) * nodes],
            held[pair, c],
            (((1,), (1,)), ((), ())),
            preferred_element_type=jnp.float32,
        )
        total = term if total is None else total + term
    value = (total * scale).astype(jnp.bfloat16)
    for i in range(out.shape[0]):
        out[i] = value


def column_for_all(acts, flat, copies, scale):
    vmem = pl.BlockSpec(memory_space=pltpu.VMEM)
    features = acts[0].shape[1]
    return pl.pallas_call(
        functools.partial(column_kernel, scale),
        out_shape=jax.ShapeDtypeStruct((copies, flat.shape[0], features), jnp.bfloat16),
        in_specs=[pl.BlockSpec(memory_space=pl.ANY)] * len(acts) + [vmem],
        out_specs=vmem,
        scratch_shapes=[
            pltpu.VMEM((len(acts), *acts[0].shape), acts[0].dtype),
            pltpu.SemaphoreType.DMA((len(acts),)),
        ],
        compiler_params=pltpu.CompilerParams(vmem_limit_bytes=16 * 1024 * 1024),
        cost_estimate=pl.CostEstimate(
            flops=2 * features * flat.size, bytes_accessed=2 * features * flat.shape[1], transcendentals=0
        ),
        name="column",
    )(*acts, flat)


def sent_to_all(shard, axis):
    size = lax.axis_size(axis)
    return lax.all_to_all(
        jnp.broadcast_to(shard[None], (size, *shard.shape)), axis, 0, 0, tiled=True
    )


def per_device(out_grad, pre_act, in_act, weight, tiles, indices, counts):
    feats, local_nodes = out_grad.shape
    _, _, blk, _ = tiles.shape
    parts, nodes = lax.axis_size("feat"), lax.axis_size("node")
    assert nodes == RING[0] * RING[1] and parts == FEAT[0] * FEAT[1]
    grad_pre = jnp.where(pre_act > 0, out_grad, jnp.zeros_like(out_grad))
    own = grad_pre.reshape(feats, local_nodes // blk, blk).transpose(1, 0, 2)
    pieces = gathered(own)
    me = lax.axis_index("feat")
    spot = lax.axis_index("node")
    y, core = me // FEAT[1], me % FEAT[1]
    here = jnp.stack([y, core, spot // RING[1], spot % RING[1]]).astype(jnp.int32)
    both = jnp.stack([in_act, over_feat(in_act, 0, 1)])
    acts = [both] + [over_feat(both, -s, 0) for s in range(1, FEAT[0])]
    turned = jnp.concatenate(
        [
            lax.dynamic_slice_in_dim(
                weight,
                (lax.rem(y + FEAT[0] - s, FEAT[0]) * FEAT[1] + lax.rem(core + c, FEAT[1])) * feats,
                feats,
                1,
            )
            for s in range(FEAT[0])
            for c in range(FEAT[1])
        ],
        axis=1,
    )
    keep, cross, flat = gathered_sum(here, counts, indices, tiles, pieces, parts)

    scale = float(local_nodes * nodes) ** (-0.5)
    everyone = lax.all_to_all(
        column_for_all(acts, flat, nodes, scale), "node", 0, 0, tiled=True
    )
    column = jnp.sum(everyone.astype(jnp.float32), axis=0)
    columns = sent_to_all(column.astype(jnp.bfloat16), "feat")
    weight_grad = columns.reshape(-1, column.shape[1]).T.astype(jnp.float32)

    crossed = over_feat(cross, 0, 1)
    ready = [jnp.concatenate([keep[s], crossed[s]], axis=0) for s in range(FEAT[0])]
    received = [ready[0]] + [over_feat(ready[s], s, 0) for s in range(1, FEAT[0])]
    node_rows = jnp.concatenate(received, axis=0)
    in_grad = jnp.dot(turned, node_rows, preferred_element_type=jnp.float32).astype(jnp.bfloat16)
    return in_grad, weight_grad


def solution(mesh):
    in_specs = (
        P("feat", "node"),
        P("feat", "node"),
        P(None, ("node", "feat")),
        P(),
        P("node", None, None, None),
        P("node", None),
        P("node"),
    )
    out_specs = (P(None, ("node", "feat")), P())

    return jax.shard_map(
        per_device, mesh=mesh, in_specs=in_specs, out_specs=out_specs, check_vma=False
    )
```

```python
import collections
import functools

import jax
import jax.numpy as jnp
from jax import lax
from jax.experimental import pallas as pl
from jax.experimental.pallas import tpu as pltpu
from jax.sharding import PartitionSpec as P


RING = (8, 4)
FEAT = (4, 2)
SPLIT = 38
GROUPS = [("gb", (1,), True), ("gc", (2,), False), ("gd", (3, 4), True)]
UPPER = 33

QUAD = 8
GROUP = 8
DEPTH = 3


def plan_kernel(counts, work, length):
    rows = counts.shape[0]

    def one_row(r, n):
        runs = (counts[r] + QUAD - 1) // QUAD

        def one_run(c, n):
            work[n] = r * 32 + c * QUAD
            return n + 1

        return lax.fori_loop(0, runs, one_run, n)

    n = lax.fori_loop(0, rows, one_row, 0)
    length[0] = n
    for j in range(GROUP):
        work[n + j] = rows * 32


def make_plan(counts, slots):
    rows = counts.shape[0]
    smem = pl.BlockSpec(memory_space=pltpu.SMEM)
    return pl.pallas_call(
        plan_kernel,
        out_shape=(
            jax.ShapeDtypeStruct((rows * slots // QUAD + GROUP,), jnp.int32),
            jax.ShapeDtypeStruct((1,), jnp.int32),
        ),
        in_specs=[smem],
        out_specs=(smem, smem),
        name="plan",
    )(counts)


def gather_kernel(
    runs, here, work, length, counts, indices, tiles, *rest
):
    pieces = rest[: len(runs)]
    keep, cross, flat, held, stream, total, held_sem, stream_sem = rest[len(runs) :]
    rows, blk = counts.shape[0], tiles.shape[1]
    slots = tiles.shape[0] // rows
    groups = (length[0] + GROUP - 1) // GROUP
    shard = held.shape[0] // (RING[0] * RING[1])
    for piece, inside in zip(pieces, runs):
        start = 0
        for n, dz, dx, at in inside:
            z = lax.rem(here[2] + dz % RING[0], RING[0])
            x = lax.rem(here[3] + dx % RING[1], RING[1])
            place = (z * RING[1] + x) * shard + at
            pltpu.make_async_copy(
                piece.at[pl.ds(start, n)], held.at[pl.ds(place, n)], held_sem
            ).start()
            start += n

    def fetch(group):
        slot = lax.rem(group, DEPTH)
        for j in range(GROUP):
            entry = work[group * GROUP + j]
            r = jnp.minimum(lax.shift_right_logical(entry, 5), rows - 1)
            k = entry & 31
            pltpu.make_async_copy(
                tiles.at[pl.ds(r * slots + k, QUAD)], stream.at[slot, pl.ds(j * QUAD, QUAD)], stream_sem.at[slot]
            ).start()

    for g in range(DEPTH - 1):
        @pl.when(g < groups)
        def _():
            fetch(g)

    total[...] = jnp.zeros_like(total)
    pltpu.make_async_copy(held, held, held_sem).wait()

    def one_group(group, carry):
        @pl.when(group + DEPTH - 1 < groups)
        def _():
            fetch(group + DEPTH - 1)

        slot = lax.rem(group, DEPTH)
        pltpu.make_async_copy(
            tiles.at[pl.ds(0, GROUP * QUAD)], stream.at[slot], stream_sem.at[slot]
        ).wait()
        terms, where = [], []
        for j in range(GROUP):
            entry = work[group * GROUP + j]
            r = lax.shift_right_logical(entry, 5)
            k = entry & 31
            row = jnp.minimum(r, rows - 1)
            live = jnp.where(r < rows, counts[row], 0)
            picked = []
            for q in range(QUAD):
                block = held[indices[row * slots + k + q]]
                picked.append(jnp.where(k + q < live, block, jnp.zeros_like(block)))
            picked = jnp.concatenate(picked, axis=1)
            weights = jnp.concatenate([stream[slot, j * QUAD + q] for q in range(QUAD)], axis=1)
            terms.append(
                lax.dot_general(
                    picked, weights, (((1,), (1,)), ((), ())), preferred_element_type=jnp.float32
                )
            )
            where.append(r)
        for j in range(GROUP):
            total[where[j]] += terms[j]
        return carry

    lax.fori_loop(0, groups, one_group, 0)

    nodes = keep.shape[2]
    per_part = nodes // blk

    def one_step(s, carry):
        for c, out in enumerate((keep, cross)):
            part = lax.rem(here[0] + s, FEAT[0]) * FEAT[1] + lax.rem(here[1] + c, FEAT[1])
            for i in range(per_part):
                value = total[part * per_part + i].astype(jnp.bfloat16)
                out[s, :, i * blk : (i + 1) * blk] = value
                at = pl.multiple_of((s * FEAT[1] + c) * nodes + i * blk, blk)
                flat[:, pl.ds(at, blk)] = value
        return carry

    lax.fori_loop(0, FEAT[0], one_step, 0)


def gathered_sum(here, counts, indices, tiles, pieces, parts):
    rows, slots, blk, _ = tiles.shape
    feats = pieces[0].blocks.shape[1]
    total_blocks = sum(p.blocks.shape[0] for p in pieces)
    smem = pl.BlockSpec(memory_space=pltpu.SMEM)
    vmem = pl.BlockSpec(memory_space=pltpu.VMEM)
    anywhere = pl.BlockSpec(memory_space=pl.ANY)
    out_shape = (
        jax.ShapeDtypeStruct((FEAT[0], feats, rows * blk // parts), jnp.bfloat16),
        jax.ShapeDtypeStruct((FEAT[0], feats, rows * blk // parts), jnp.bfloat16),
        jax.ShapeDtypeStruct((feats, rows * blk), jnp.bfloat16),
    )
    work, length = make_plan(counts, slots)
    work_done = rows * slots // 2
    return pl.pallas_call(
        functools.partial(gather_kernel, [p.runs for p in pieces]),
        out_shape=out_shape,
        in_specs=[smem] * 5 + [anywhere] * (1 + len(pieces)),
        out_specs=(vmem, vmem, vmem),
        scratch_shapes=[
            pltpu.VMEM((total_blocks, feats, blk), pieces[0].blocks.dtype),
            pltpu.VMEM((DEPTH, GROUP * QUAD, blk, blk), tiles.dtype),
            pltpu.VMEM((rows + 1, feats, blk), jnp.float32),
            pltpu.SemaphoreType.DMA,
            pltpu.SemaphoreType.DMA((DEPTH,)),
        ],
        compiler_params=pltpu.CompilerParams(vmem_limit_bytes=48 * 1024 * 1024),
        cost_estimate=pl.CostEstimate(
            flops=2 * work_done * feats * blk * blk,
            bytes_accessed=2 * work_done * blk * blk + 2 * total_blocks * feats * blk,
            transcendentals=0,
        ),
        name="gathered_sum",
    )(
        here,
        work,
        length,
        counts,
        indices.reshape(-1),
        tiles.reshape(rows * slots, blk, blk),
        *(p.blocks for p in pieces),
    )


Piece = collections.namedtuple("Piece", "blocks runs")


def hop(piece, dz, dx):
    nz, nx = RING
    pairs = [
        (z * nx + x, (z + dz) % nz * nx + (x + dx) % nx) for z in range(nz) for x in range(nx)
    ]
    blocks = lax.ppermute(piece.blocks, "node", pairs)
    return Piece(blocks, [(n, z - dz, x - dx, at) for n, z, x, at in piece.runs])


def cut(piece, low, high):
    runs, seen = [], 0
    for n, z, x, at in piece.runs:
        first, last = max(low, seen), min(high, seen + n)
        if first < last:
            runs.append((last - first, z, x, at + first - seen))
        seen += n
    return Piece(piece.blocks[low:high], runs)


def join(*pieces):
    return Piece(
        jnp.concatenate([p.blocks for p in pieces], axis=0), [r for p in pieces for r in p.runs]
    )


def along(axis, piece, steps, upper):
    dz, dx = (1, 0) if axis == "z" else (0, 1)
    up = down = piece
    size = piece.blocks.shape[0]
    out = []
    for s in range(1, steps + 1):
        if s == steps and upper < size:
            down = cut(down, upper, size) if upper else down
            up = cut(up, 0, upper) if upper else None
        elif s == steps:
            down = None
        step = []
        if up is not None:
            up = hop(up, dz, dx)
            step.append(up)
        if down is not None:
            down = hop(down, -dz, -dx)
            step.append(down)
        out.append(step)
    return out


def gathered(own):
    shard = own.shape[0]
    a = Piece(own[:SPLIT], [(SPLIT, 0, 0, 0)])
    b = Piece(own[SPLIT:], [(shard - SPLIT, 0, 0, SPLIT)])
    az = along("z", a, RING[0] // 2, SPLIT)
    bx = along("x", b, RING[1] // 2, shard - SPLIT)
    across = join(b, *bx[0], *bx[1])
    pieces = [a, across]
    groups = [("ga", a, False)]
    for name, steps, one_way in GROUPS:
        joined = join(*(p for s in steps for p in az[s - 1]))
        groups.append((name, joined, one_way))
        pieces.append(joined)
    for name, piece, one_way in groups:
        for step in along("x", piece, RING[1] // 2, piece.blocks.shape[0] if one_way else 0):
            pieces += step
    for step in along("z", across, RING[0] // 2, UPPER):
        pieces += step
    return pieces


def over_feat(value, steps, swap):
    ny, nc = FEAT
    pairs = [
        (y * nc + c, (y + steps) % ny * nc + (c + swap) % nc) for y in range(ny) for c in range(nc)
    ]
    return lax.ppermute(value, "feat", pairs)


def column_kernel(scale, *refs):
    acts, flat, out = refs[:-2], refs[-2], refs[-1]
    nodes = acts[0].shape[2]
    total = None
    for s in range(len(acts) * acts[0].shape[0]):
        pair, c = s // acts[0].shape[0], s % acts[0].shape[0]
        term = lax.dot_general(
            flat[:, s * nodes : (s + 1) * nodes],
            acts[pair][c],
            (((1,), (1,)), ((), ())),
            preferred_element_type=jnp.float32,
        )
        total = term if total is None else total + term
    value = (total * scale).astype(jnp.bfloat16)
    for i in range(out.shape[0]):
        out[i] = value


def column_for_all(acts, flat, copies, scale):
    vmem = pl.BlockSpec(memory_space=pltpu.VMEM)
    features = acts[0].shape[1]
    return pl.pallas_call(
        functools.partial(column_kernel, scale),
        out_shape=jax.ShapeDtypeStruct((copies, flat.shape[0], features), jnp.bfloat16),
        in_specs=[vmem] * (len(acts) + 1),
        out_specs=vmem,
        compiler_params=pltpu.CompilerParams(vmem_limit_bytes=16 * 1024 * 1024),
        cost_estimate=pl.CostEstimate(
            flops=2 * features * flat.size, bytes_accessed=2 * features * flat.shape[1], transcendentals=0
        ),
        name="column",
    )(*acts, flat)


def sent_to_all(shard, axis):
    size = lax.axis_size(axis)
    return lax.all_to_all(
        jnp.broadcast_to(shard[None], (size, *shard.shape)), axis, 0, 0, tiled=True
    )


def per_device(out_grad, pre_act, in_act, weight, tiles, indices, counts):
    feats, local_nodes = out_grad.shape
    _, _, blk, _ = tiles.shape
    parts, nodes = lax.axis_size("feat"), lax.axis_size("node")
    assert nodes == RING[0] * RING[1] and parts == FEAT[0] * FEAT[1]
    grad_pre = jnp.where(pre_act > 0, out_grad, jnp.zeros_like(out_grad))
    own = grad_pre.reshape(feats, local_nodes // blk, blk).transpose(1, 0, 2)
    pieces = gathered(own)
    me = lax.axis_index("feat")
    spot = lax.axis_index("node")
    y, core = me // FEAT[1], me % FEAT[1]
    here = jnp.stack([y, core, spot // RING[1], spot % RING[1]]).astype(jnp.int32)
    both = jnp.stack([in_act, over_feat(in_act, 0, 1)])
    acts = [both] + [over_feat(both, -s, 0) for s in range(1, FEAT[0])]
    turned = jnp.concatenate(
        [
            lax.dynamic_slice_in_dim(
                weight,
                (lax.rem(y + FEAT[0] - s, FEAT[0]) * FEAT[1] + lax.rem(core + c, FEAT[1])) * feats,
                feats,
                1,
            )
            for s in range(FEAT[0])
            for c in range(FEAT[1])
        ],
        axis=1,
    )
    keep, cross, flat = gathered_sum(here, counts, indices, tiles, pieces, parts)

    scale = float(local_nodes * nodes) ** (-0.5)
    everyone = lax.all_to_all(
        column_for_all(acts, flat, nodes, scale), "node", 0, 0, tiled=True
    )
    column = jnp.sum(everyone.astype(jnp.float32), axis=0)
    columns = sent_to_all(column.astype(jnp.bfloat16), "feat")
    weight_grad = columns.reshape(-1, column.shape[1]).T.astype(jnp.float32)

    crossed = over_feat(cross, 0, 1)
    ready = [jnp.concatenate([keep[s], crossed[s]], axis=0) for s in range(FEAT[0])]
    received = [ready[0]] + [over_feat(ready[s], s, 0) for s in range(1, FEAT[0])]
    node_rows = jnp.concatenate(received, axis=0)
    in_grad = jnp.dot(turned, node_rows, preferred_element_type=jnp.float32).astype(jnp.bfloat16)
    return in_grad, weight_grad


def solution(mesh):
    in_specs = (
        P("feat", "node"),
        P("feat", "node"),
        P(None, ("node", "feat")),
        P(),
        P("node", None, None, None),
        P("node", None),
        P("node"),
    )
    out_specs = (P(None, ("node", "feat")), P())

    return jax.shard_map(
        per_device, mesh=mesh, in_specs=in_specs, out_specs=out_specs, check_vma=False
    )
```
